256 devices in a mesh: tok: 64 (over z, x, core), head: 4 (over y).
Axes of the slice: x: 4, y: 4, z: 8, core: 2. Of those that a mesh axis runs over, the one named last changes fastest.
Arguments:
- single: bfloat16 [2048, 768], P('tok'), may hold values from -6 to 6
- pair: bfloat16 [2048, 2048, 128], P('tok', 'head'), may hold values from -161 to 161
- atoms: bfloat16 [49152, 128], P('tok'), may hold values from -60 to 60
- atom_counts: int32 [2048], P('tok'), may hold values from 4 to 24, as said below
- w_atom: bfloat16 [128, 3, 128], P(None, None, 'head'), may hold values from -0.5 to 0.5
- w_atom_token: bfloat16 [128, 768], P('head'), may hold values from -6 to 6
- ln_gain: bfloat16 [768], replicated, may hold values from 0.099609375 to 1.8984375
- w_proj: bfloat16 [768, 4, 768], P(None, None, 'head'), may hold values from -0.21875 to 0.21875
- w_pair_bias: bfloat16 [128, 16], replicated, may hold values from -3.5 to 3.5
- w_out: bfloat16 [768, 768], P('head'), may hold values from -0.21875 to 0.21875
- ln_gain2: bfloat16 [768], replicated, may hold values from 0.099609375 to 1.8984375
- w_trans: bfloat16 [768, 2, 1536], P(None, None, 'head'), may hold values from -0.21875 to 0.21875
- w_trans_out: bfloat16 [1536, 768], P('head'), may hold values from -0.15625 to 0.15625
Outputs:
- refined: bfloat16 [2048, 768], P('tok', 'head')
- atom_mix: bfloat16 [128, 49152], P('head', 'tok')
The draws below stay inside these ranges and needn't reach their ends.
Inputs may be any that keep to these rules, and one draw needn't show every extreme that they name: `atom_counts`: every token has 4 to 24 atoms; in every draw all tokens of some group of 32 have 24 atoms.
All inputs are finite; a program needn't handle non-finite values.
Results may differ from the reference program's by a relative error of at most 0.013.
Values may be sent and summed in bfloat16 or wider, within the bound.
No kernel may reach another device: no remote copies, remote signals or barrier semaphores. Data moves between devices by JAX's collectives and lax.ppermute only.
A program may use at most 64 MiB of HBM per device.

```python
import jax
import jax.numpy as jnp
from jax import lax

D = 768
H = 16
CZ = 128
ATOM_WIDTH = 128
AH = 4
FF = 1536
TOK_DEV = 32
QWIN = 32
KWIN = 128
MINA = 4
MAXA = 24
NTOK = 2048
ACAP = 768
SLOTS_TOTAL = 49152


def draw_atom_counts(key, part):
    group_list = NTOK // TOK_DEV
    level_key = jax.random.fold_in(key, 11)
    token_key = jax.random.fold_in(key, 12)
    full_key = jax.random.fold_in(key, 13)
    levels = jax.random.randint(level_key, (group_list, 1), MINA, MAXA + 1)
    random_bits = jax.random.randint(token_key, (group_list, TOK_DEV), 0, 1 << 20)
    counts = MINA + random_bits % (levels - MINA + 1)
    full_group = jax.random.randint(full_key, (), 0, group_list)
    counts = jnp.where(jnp.arange(group_list)[:, None] == full_group, MAXA, counts)
    return counts.reshape(NTOK).astype(jnp.int32)


def draw_pair(key, part):
    starting_key = jax.random.fold_in(key, 21)
    value_entries = jnp.clip(jax.random.normal(starting_key, (NTOK, NTOK, CZ), jnp.float32), -6.0, 6.0)
    return value_entries.astype(jnp.bfloat16)


def draw_atoms(key, part):
    starting_key = jax.random.fold_in(key, 31)
    value_entries = jnp.clip(jax.random.normal(starting_key, (SLOTS_TOTAL, ATOM_WIDTH), jnp.float32), -6.0, 6.0)
    return value_entries.astype(jnp.bfloat16)


def steps_of(own_key, shape, pieces, smallest, high):
    level, own = 1.0, jax.random.fold_in(own_key, 6)
    for position, blocks in pieces:
        heights = jnp.exp(jax.random.uniform(jax.random.fold_in(own, position), (blocks,), jnp.float32, smallest / len(pieces), high / len(pieces)))
        level = level * jnp.repeat(heights, shape[position] // blocks).reshape([-1 if axis == position else 1 for axis in range(len(shape))])
    return level


def bell_draw(rng, shape, deviation, limit, shards=(), held_as=jnp.bfloat16):
    values = deviation * jax.random.normal(rng, shape, jnp.float32)
    if shards:
        values = values * steps_of(rng, shape, shards, -0.22, 0.18)
    return jnp.clip(values, -limit, limit).astype(held_as)


def setup_inputs(seed: int = 0) -> dict:
    splits = jax.random.split(jax.random.key(seed), 14)
    return {
        "single": bell_draw(splits[0], (NTOK, D), 1.0, 6.0, ((0, 64),)),
        "pair": draw_pair(jax.random.fold_in(splits[13], 71), 0),
        "atoms": draw_atoms(jax.random.fold_in(splits[13], 71), 0),
        "atom_counts": draw_atom_counts(jax.random.fold_in(splits[13], 71), 0),
        "w_atom": bell_draw(splits[4], (ATOM_WIDTH, 3, ATOM_WIDTH), ATOM_WIDTH ** -0.5, 0.5, ((2, 4),)),
        "w_atom_token": bell_draw(splits[5], (ATOM_WIDTH, D), 1.0, 6.0, ((0, 4),)),
        "ln_gain": jnp.clip(1.0 + 0.18 * jax.random.normal(splits[6], (D,), jnp.float32), 0.099609375, 1.8984375).astype(jnp.bfloat16),
        "w_proj": bell_draw(splits[7], (D, 4, D), D ** -0.5, 0.21875, ((2, 4),)),
        "w_pair_bias": bell_draw(splits[8], (CZ, H), 0.22, 3.5),
        "w_out": bell_draw(splits[9], (D, D), D ** -0.5, 0.21875, ((0, 4),)),
        "ln_gain2": jnp.clip(1.0 + 0.18 * jax.random.normal(splits[10], (D,), jnp.float32), 0.099609375, 1.8984375).astype(jnp.bfloat16),
        "w_trans": bell_draw(splits[11], (D, 2, FF), D ** -0.5, 0.21875, ((2, 4),)),
        "w_trans_out": bell_draw(splits[12], (FF, D), FF ** -0.5, 0.15625, ((0, 4),)),
    }


norm_eps = 1e-05
masked_value = -1000000000.0

def layer_norm(value_entries, gain):
    average = lax.optimization_barrier(jnp.mean(value_entries, axis=-1, keepdims=True))
    centred = value_entries - average
    spread = lax.optimization_barrier(jnp.mean(centred * centred, axis=-1, keepdims=True))
    return centred * lax.rsqrt(spread + norm_eps) * gain.astype(jnp.float32)

def group_layout(atom_counts):
    counts = atom_counts.reshape(NTOK // TOK_DEV, TOK_DEV).astype(jnp.int32)
    starts = (jnp.cumsum(counts, axis=1) - counts).astype(jnp.int32)
    totals = lax.optimization_barrier(jnp.sum(counts, axis=1)).astype(jnp.int32)
    return (counts, starts, totals)

def atom_attention(atoms, atom_counts, w_atom):
    group_list = NTOK // TOK_DEV
    windows = ACAP // QWIN
    head_size = ATOM_WIDTH // AH
    tail_rows = (KWIN - QWIN) // 2
    counts, starts, totals = group_layout(atom_counts)
    start_offsets = (jnp.cumsum(totals) - totals).astype(jnp.int32)
    everything = jnp.sum(totals).astype(jnp.int32)
    projected_rows = jnp.dot(atoms, w_atom.reshape(ATOM_WIDTH, 3 * ATOM_WIDTH), preferred_element_type=jnp.float32).astype(jnp.bfloat16)
    slot_position = jnp.arange(SLOTS_TOTAL, dtype=jnp.int32)
    owning_group = slot_position // ACAP
    inner_position = slot_position % ACAP
    active_mask = inner_position < totals[owning_group]
    atom_position = jnp.where(active_mask, start_offsets[owning_group] + inner_position, SLOTS_TOTAL).astype(jnp.int32)
    packed_rows = jnp.zeros((SLOTS_TOTAL, 2 * ATOM_WIDTH), jnp.bfloat16).at[atom_position].set(projected_rows[:, ATOM_WIDTH:], mode='drop')

    def single_group(group_pos):
        block = lax.dynamic_slice_in_dim(projected_rows, group_pos * ACAP, ACAP, 0)
        queries = block[:, :ATOM_WIDTH].reshape(windows, QWIN, AH, head_size).astype(jnp.float32)
        local_pos = jnp.arange(windows, dtype=jnp.int32)[:, None] * QWIN + jnp.arange(KWIN, dtype=jnp.int32)[None, :] - tail_rows
        target_index = start_offsets[group_pos] + local_pos
        key_valid = (target_index >= 0) & (target_index < everything)
        loaded_rows = packed_rows[jnp.clip(target_index, 0, SLOTS_TOTAL - 1)]
        key_rows = loaded_rows[:, :, :ATOM_WIDTH].reshape(windows, KWIN, AH, head_size).astype(jnp.float32)
        value_rows = loaded_rows[:, :, ATOM_WIDTH:].reshape(windows, KWIN, AH, head_size).astype(jnp.float32)
        scores = jnp.einsum('wqhd,wkhd->whqk', queries, key_rows) * head_size ** (-0.5)
        scores = jnp.where(key_valid[:, None, None, :], scores, masked_value)
        row_max = lax.optimization_barrier(jnp.max(scores, axis=-1, keepdims=True))
        lifted = jnp.exp(scores - row_max)
        weights = (lifted / lax.optimization_barrier(jnp.sum(lifted, axis=-1, keepdims=True))).astype(jnp.bfloat16)
        mixed = jnp.einsum('whqk,wkhd->wqhd', weights.astype(jnp.float32), value_rows)
        query_live = (jnp.arange(ACAP, dtype=jnp.int32) < totals[group_pos]).reshape(windows, QWIN)
        mixed = jnp.where(query_live[:, :, None, None], mixed, 0.0)
        return mixed.reshape(ACAP, ATOM_WIDTH).astype(jnp.bfloat16)
    return lax.map(single_group, jnp.arange(group_list, dtype=jnp.int32)).reshape(SLOTS_TOTAL, ATOM_WIDTH)

def token_means(atom_out, atom_counts):
    group_list = NTOK // TOK_DEV
    counts, starts, totals = group_layout(atom_counts)
    slot_position = jnp.arange(ACAP, dtype=jnp.int32)
    member = (slot_position[None, None, :] >= starts[:, :, None]) & (slot_position[None, None, :] < (starts + counts)[:, :, None])
    member = member.astype(jnp.float32)
    totals_rows = jnp.einsum('gts,gsc->gtc', member, atom_out.reshape(group_list, ACAP, ATOM_WIDTH).astype(jnp.float32))
    return (totals_rows / counts[:, :, None].astype(jnp.float32)).reshape(NTOK, ATOM_WIDTH)

def reference(single, pair, atoms, atom_counts, w_atom, w_atom_token, ln_gain, w_proj, w_pair_bias, w_out, ln_gain2, w_trans, w_trans_out):
    atom_out = atom_attention(atoms, atom_counts, w_atom)
    token_atoms = token_means(atom_out, atom_counts).astype(jnp.bfloat16)
    residual_state = single.astype(jnp.float32) + jnp.dot(token_atoms, w_atom_token, preferred_element_type=jnp.float32)
    normed = layer_norm(residual_state, ln_gain).astype(jnp.bfloat16)
    projected_rows = jnp.dot(normed, w_proj.reshape(D, 4 * D), preferred_element_type=jnp.float32).reshape(NTOK, 4, D)
    queries = projected_rows[:, 0].astype(jnp.bfloat16)
    key_rows = projected_rows[:, 1].astype(jnp.bfloat16)
    value_rows = projected_rows[:, 2].astype(jnp.bfloat16)
    gate_raw = projected_rows[:, 3]
    pair_term = jnp.dot(pair.reshape(NTOK * NTOK, CZ), w_pair_bias, preferred_element_type=jnp.float32).astype(jnp.bfloat16)
    pair_term = jnp.transpose(pair_term.reshape(NTOK, NTOK, H), (2, 0, 1))
    head_size = D // H

    def one_head(head_pos):
        query_head = lax.dynamic_slice_in_dim(queries, head_pos * head_size, head_size, 1)
        key_head = lax.dynamic_slice_in_dim(key_rows, head_pos * head_size, head_size, 1)
        value_head = lax.dynamic_slice_in_dim(value_rows, head_pos * head_size, head_size, 1)
        pair_head = lax.dynamic_index_in_dim(pair_term, head_pos, 0, keepdims=False)
        scores = jnp.dot(query_head, key_head.T, preferred_element_type=jnp.float32) * head_size ** (-0.5)
        scores = scores + pair_head.astype(jnp.float32)
        row_max = lax.optimization_barrier(jnp.max(scores, axis=-1, keepdims=True))
        lifted = jnp.exp(scores - row_max)
        weights = (lifted / lax.optimization_barrier(jnp.sum(lifted, axis=-1, keepdims=True))).astype(jnp.bfloat16)
        return jnp.dot(weights, value_head, preferred_element_type=jnp.float32)
    context = lax.map(one_head, jnp.arange(H, dtype=jnp.int32))
    context = jnp.transpose(context, (1, 0, 2)).reshape(NTOK, D)
    gated_rows = (context * jax.nn.sigmoid(gate_raw)).astype(jnp.bfloat16)
    state_after = residual_state + jnp.dot(gated_rows, w_out, preferred_element_type=jnp.float32)
    normed_after = layer_norm(state_after, ln_gain2).astype(jnp.bfloat16)
    gate_up = jnp.dot(normed_after, w_trans.reshape(D, 2 * FF), preferred_element_type=jnp.float32)
    hidden = (jax.nn.silu(gate_up[:, :FF]) * gate_up[:, FF:]).astype(jnp.bfloat16)
    refined = (state_after + jnp.dot(hidden, w_trans_out, preferred_element_type=jnp.float32)).astype(jnp.bfloat16)
    return (refined, atom_out.T)
```

```python
import jax
import jax.numpy as jnp
from jax import lax
from jax.experimental import pallas as pl
from jax.experimental.pallas import tpu as pltpu
from jax.sharding import Mesh
from jax.sharding import PartitionSpec as P

H = 16
AH = 4
QWIN = 32
KWIN = 128
TAIL = (KWIN - QWIN) // 2
HEADROWS = (KWIN + QWIN) // 2
QBLOCK = 128
KBLOCK = QBLOCK + KWIN

norm_eps = 1e-05
masked_value = -1000000000.0
f32 = jnp.float32
bf16 = jnp.bfloat16
NT = (((1,), (1,)), ((), ()))
TOK = ("z", "x", "core")


def sent_around(block, axis, distance):
    size = lax.axis_size(axis)
    return lax.ppermute(block, axis, [(i, (i + distance) % size) for i in range(size)])


def from_behind(block, axis, distance):
    devices = range(lax.axis_size(axis))
    route = [(i - distance, i) for i in devices if i - distance in devices]
    return lax.ppermute(block, axis, route)


def of_everyone(partial):
    return [partial] + [sent_around(partial, "head", d) for d in (1, 2, 3)]


def exchanged(pieces, axis):
    return lax.all_to_all(pieces, axis, split_axis=0, concat_axis=0, tiled=True)


def live_atoms(count_ref):
    live = count_ref[0]
    for i in range(1, count_ref.shape[0]):
        live = live + count_ref[i]
    return live


def layer_norm(value, gain):
    average = jnp.mean(value, axis=-1, keepdims=True)
    centred = value - average
    spread = jnp.mean(centred * centred, axis=-1, keepdims=True)
    return centred * lax.rsqrt(spread + norm_eps) * gain


def halo_kernel(count_ref, atoms, head_rows, tail_rows, rows):
    live = live_atoms(count_ref)
    rows[...] = atoms[...].astype(f32)
    head_rows[...] = atoms[0:HEADROWS]
    tail_rows[...] = rows[pl.ds(live - TAIL, TAIL), :].astype(bf16)


def pair_kernel(pair, w_bias, out):
    half = pair.shape[1] // 2
    w = w_bias[...].astype(f32)
    blank = jnp.zeros_like(w)
    both = jnp.concatenate(
        [jnp.concatenate([w, blank], axis=1), jnp.concatenate([blank, w], axis=1)], axis=0
    ).astype(bf16)
    terms = []
    for q in range(pair.shape[0]):
        keys = jnp.concatenate([pair[q, :half], pair[q, half:]], axis=1)
        term = lax.dot_general(both, keys, NT, preferred_element_type=f32)
        terms.append(jnp.concatenate([term[:H], term[H:]], axis=1))
    out[...] = jnp.stack(terms, axis=1).astype(bf16)


def atom_kernel(
    where_ref, count_ref, counts_row, atoms, previous, following, w_atom, w_token, partial, mix, rows
):
    slots = atoms.shape[0]
    tokens = counts_row.shape[1]
    width = w_token.shape[0]
    live = live_atoms(count_ref)
    first = where_ref[0] == 0
    last = where_ref[0] == where_ref[1]
    rows[0:TAIL] = previous[...].astype(f32)
    rows[TAIL : TAIL + slots] = atoms[...].astype(f32)
    rows[TAIL + slots :] = jnp.zeros((HEADROWS, atoms.shape[1]), f32)
    rows[pl.ds(TAIL + live, HEADROWS), :] = following[...].astype(f32)
    keyed = rows[...].astype(bf16)

    def projected(part):
        w = w_atom[part * width : (part + 1) * width, :]
        return lax.dot_general(keyed, w, NT, preferred_element_type=f32)

    queries = projected(0)[TAIL : TAIL + slots].astype(bf16)
    keys = projected(1).astype(bf16)
    values = projected(2).astype(bf16)

    counts = jnp.broadcast_to(counts_row[...].astype(f32), (tokens, tokens))
    token_row = lax.broadcasted_iota(jnp.int32, (tokens, tokens), 0)
    token_lane = lax.broadcasted_iota(jnp.int32, (tokens, tokens), 1)
    starts = jnp.sum(jnp.where(token_lane < token_row, counts, 0.0), axis=1, keepdims=True)
    own = jnp.sum(jnp.where(token_lane == token_row, counts, 0.0), axis=1, keepdims=True)

    row = lax.broadcasted_iota(jnp.int32, (QBLOCK, KBLOCK), 0)
    lane = lax.broadcasted_iota(jnp.int32, (QBLOCK, KBLOCK), 1)
    offset = lane - (row // QWIN) * QWIN
    in_window = (offset >= 0) & (offset < KWIN)
    low = jnp.where(first, 0, -slots)
    high = jnp.where(last, live, 4 * slots)
    out_row = lax.broadcasted_iota(jnp.int32, (QBLOCK, width), 0)
    slot = lax.broadcasted_iota(jnp.int32, (tokens, QBLOCK), 1).astype(f32)
    totals = jnp.zeros((tokens, width), f32)
    for b in range(slots // QBLOCK):
        at = b * QBLOCK
        scores = lax.dot_general(
            queries[at : at + QBLOCK], keys[at : at + KBLOCK], NT, preferred_element_type=f32
        ) * width ** (-0.5)
        key_pos = lane + (at - TAIL)
        scores = jnp.where(in_window & (key_pos >= low) & (key_pos < high), scores, masked_value)
        lifted = jnp.exp(scores - jnp.max(scores, axis=1, keepdims=True))
        weights = (lifted / jnp.sum(lifted, axis=1, keepdims=True)).astype(bf16)
        out = jnp.dot(weights, values[at : at + KBLOCK], preferred_element_type=f32)
        out = jnp.where(out_row + at < live, out, 0.0)
        mix[:, at : at + QBLOCK] = out.T.astype(bf16)
        member = (slot + at >= starts) & (slot + at < starts + own)
        totals = totals + jnp.dot(
            jnp.where(member, 1.0, 0.0).astype(bf16), out.astype(bf16), preferred_element_type=f32
        )
    token_atoms = (totals / own).astype(bf16)
    partial[...] = jnp.dot(token_atoms, w_token[...], preferred_element_type=f32).astype(bf16)


def projection_kernel(p0, p1, p2, p3, single, gain, w_proj, residual, kv, query, gate):
    term = (p0[...].astype(f32) + p1[...].astype(f32)) + (p2[...].astype(f32) + p3[...].astype(f32))
    state = single[...].astype(f32) + term
    residual[...] = state
    normed = layer_norm(state, gain[...].astype(f32)).astype(bf16)
    own = lax.dot_general(normed, w_proj[...], NT, preferred_element_type=f32)
    part = own.shape[1] // 4
    query[...] = own[:, :part].astype(bf16)
    gate[...] = own[:, 3 * part :]
    pair = jnp.concatenate([own[:, 2 * part : 3 * part], own[:, part : 2 * part]], axis=1).astype(bf16)
    for i in range(kv.shape[0]):
        kv[i] = pair


def attention_kernel(where_ref, kv_own, kv_other, query, gate, bias, w_out, partial, kv, scores):
    core = where_ref[2]
    groups, tokens, width = kv_own.shape
    kv[:, pl.ds(core, 1)] = kv_own[...].reshape(groups, 1, tokens, width)
    kv[:, pl.ds(1 - core, 1)] = kv_other[...].reshape(groups, 1, tokens, width)
    part = query.shape[1]
    size = part // 4
    rows = 4 * tokens
    reach = 256
    blank = jnp.zeros((tokens, reach - part), f32)
    spread = jnp.concatenate([blank, query[...].astype(f32)], axis=1)
    spread = jnp.concatenate([spread] * 4, axis=0)
    head = lax.broadcasted_iota(jnp.int32, (rows, reach), 0) // tokens
    lane = lax.broadcasted_iota(jnp.int32, (rows, reach), 1) - (reach - part)
    queries = jnp.where((lane >= head * size) & (lane < (head + 1) * size), spread, 0.0)
    queries = queries.astype(bf16)
    keyed = kv[...].reshape(groups * 2 * tokens, width)
    block = bias.shape[2]
    scale = size ** (-0.5)
    top = None
    for b in range(4):
        s = lax.dot_general(
            queries,
            keyed[b * block : (b + 1) * block, width - reach :],
            NT,
            preferred_element_type=f32,
        ) * scale + bias[4 * b : 4 * b + 4].reshape(rows, block).astype(f32)
        scores[b] = s
        m = jnp.max(s, axis=1, keepdims=True)
        top = m if top is None else jnp.maximum(top, m)
    total = jnp.zeros((rows, 1), f32)
    context = jnp.zeros((rows, part), f32)
    for b in range(4):
        lifted = jnp.exp(scores[b] - top)
        total = total + jnp.sum(lifted, axis=1, keepdims=True)
        context = context + jnp.dot(
            lifted.astype(bf16),
            keyed[b * block : (b + 1) * block, :part],
            preferred_element_type=f32,
        )
    head = lax.broadcasted_iota(jnp.int32, (rows, part), 0) // tokens
    lane = lax.broadcasted_iota(jnp.int32, (rows, part), 1)
    own = (lane >= head * size) & (lane < (head + 1) * size)
    context = jnp.where(own, context / total, 0.0)
    mixed = sum(context[j * tokens : (j + 1) * tokens] for j in range(4))
    gated = (mixed * jax.nn.sigmoid(gate[...])).astype(bf16)
    partial[...] = jnp.dot(gated, w_out[...], preferred_element_type=f32).astype(bf16)


def tail_kernel(
    where_ref, p0, p1, p2, p3, residual, gain, w_trans, w_down, share, update, state
):
    term = (p0[...].astype(f32) + p1[...].astype(f32)) + (p2[...].astype(f32) + p3[...].astype(f32))
    after = residual[...] + term
    quarter = share.shape[1]
    for y in range(4):
        state[y] = after[:, y * quarter : (y + 1) * quarter]
    share[...] = state[where_ref[3]]
    normed = layer_norm(after, gain[...].astype(f32)).astype(bf16)
    gate = jnp.dot(normed, w_trans[0], preferred_element_type=f32)
    up = jnp.dot(normed, w_trans[1], preferred_element_type=f32)
    hidden = (gate * jax.nn.sigmoid(gate) * up).astype(bf16)
    moved = jnp.dot(hidden, w_down[...], preferred_element_type=f32)
    for y in range(4):
        update[y] = moved[:, y * quarter : (y + 1) * quarter].astype(bf16)


def call(kernel, out_shape, operands, scratch, smem):
    vmem = pl.BlockSpec(memory_space=pltpu.VMEM)
    scalar = pl.BlockSpec(memory_space=pltpu.SMEM)
    return pl.pallas_call(
        kernel,
        out_shape=out_shape,
        in_specs=[scalar] * smem + [vmem] * (len(operands) - smem),
        out_specs=jax.tree.map(lambda _: vmem, out_shape),
        scratch_shapes=scratch,
        compiler_params=pltpu.CompilerParams(vmem_limit_bytes=40 << 20),
        cost_estimate=pl.CostEstimate(flops=1 << 30, bytes_accessed=4 << 20, transcendentals=0),
    )(*operands)


def shards(
    single,
    pair,
    atoms,
    atom_counts,
    w_atom,
    w_atom_token,
    ln_gain,
    w_proj,
    w_pair_bias,
    w_out,
    ln_gain2,
    w_trans,
    w_trans_out,
):
    slots, channels = atoms.shape
    tokens, model = single.shape
    where_at = jnp.stack(
        [
            lax.axis_index(TOK),
            jnp.int32(lax.axis_size(TOK) - 1),
            lax.axis_index("core"),
            lax.axis_index("head"),
        ]
    ).astype(jnp.int32)
    head_rows, tail_rows = call(
        halo_kernel,
        (
            jax.ShapeDtypeStruct((HEADROWS, channels), bf16),
            jax.ShapeDtypeStruct((TAIL, channels), bf16),
        ),
        (atom_counts, atoms),
        [pltpu.VMEM((slots, channels), f32)],
        1,
    )
    pair, head_rows, tail_rows = lax.optimization_barrier((pair, head_rows, tail_rows))
    following = from_behind(head_rows, TOK, -1)
    previous = from_behind(tail_rows, TOK, 1)

    keys = pair.shape[1]
    pair_term = pl.pallas_call(
        pair_kernel,
        out_shape=jax.ShapeDtypeStruct((H, tokens, keys), bf16),
        grid=(4,),
        in_specs=[
            pl.BlockSpec((tokens // 4, keys, pair.shape[2]), lambda i: (i, 0, 0)),
            pl.BlockSpec((H, pair.shape[2]), lambda i: (0, 0)),
        ],
        out_specs=pl.BlockSpec((H, tokens // 4, keys), lambda i: (0, i, 0)),
        cost_estimate=pl.CostEstimate(flops=2 << 30, bytes_accessed=8 << 20, transcendentals=0),
    )(pair, w_pair_bias.T)
    pair_term, previous, following = lax.optimization_barrier((pair_term, previous, following))
    bias = exchanged(pair_term, "head")

    width = w_atom.shape[2]
    partial, mix = call(
        atom_kernel,
        (
            jax.ShapeDtypeStruct((tokens, model), bf16),
            jax.ShapeDtypeStruct((width, slots), bf16),
        ),
        (
            where_at,
            atom_counts,
            atom_counts.reshape(1, tokens),
            atoms,
            previous,
            following,
            w_atom.transpose(1, 2, 0).reshape(3 * width, channels),
            w_atom_token,
        ),
        [pltpu.VMEM((TAIL + slots + HEADROWS, channels), f32)],
        2,
    )
    quarter = model // 4
    residual, kv, query, gate = call(
        projection_kernel,
        (
            jax.ShapeDtypeStruct((tokens, model), f32),
            jax.ShapeDtypeStruct((32, tokens, 2 * quarter), bf16),
            jax.ShapeDtypeStruct((tokens, quarter), bf16),
            jax.ShapeDtypeStruct((tokens, quarter), f32),
        ),
        (
            *of_everyone(partial),
            single,
            ln_gain.reshape(1, model),
            w_proj.transpose(1, 2, 0).reshape(-1, model),
        ),
        [],
        0,
    )
    kv, bias = lax.optimization_barrier((kv, bias))
    kv_own = exchanged(kv, ("z", "x"))
    kv_other = sent_around(kv_own, "core", 1)
    partial = call(
        attention_kernel,
        jax.ShapeDtypeStruct((tokens, model), bf16),
        (where_at, kv_own, kv_other, query, gate, bias, w_out),
        [
            pltpu.VMEM((32, 2, tokens, 2 * quarter), bf16),
            pltpu.VMEM((4, 4 * tokens, bias.shape[2]), f32),
        ],
        1,
    )
    share, update = call(
        tail_kernel,
        (
            jax.ShapeDtypeStruct((tokens, quarter), f32),
            jax.ShapeDtypeStruct((4, tokens, quarter), bf16),
        ),
        (
            where_at,
            *of_everyone(partial),
            residual,
            ln_gain2.reshape(1, model),
            w_trans.transpose(1, 0, 2),
            w_trans_out,
        ),
        [pltpu.VMEM((4, tokens, quarter), f32)],
        1,
    )
    update = exchanged(update, "head")
    refined = (share + update.astype(f32).sum(axis=0)).astype(bf16)
    return (refined, mix)


def solution(mesh):
    devices = mesh.devices.reshape(8, 4, 2, 4)
    return jax.shard_map(
        shards,
        mesh=Mesh(devices, ("z", "x", "core", "head")),
        in_specs=(
            P(TOK, None),
            P(TOK, "head", None),
            P(TOK, None),
            P(TOK),
            P(None, None, "head"),
            P("head", None),
            P(),
            P(None, None, "head"),
            P(),
            P("head", None),
            P(),
            P(None, None, "head"),
            P("head", None),
        ),
        out_specs=(P(TOK, "head"), P("head", TOK)),
        check_vma=False,
    )
```

```python
import jax
import jax.numpy as jnp
from jax import lax
from jax.experimental import pallas as pl
from jax.experimental.pallas import tpu as pltpu
from jax.sharding import Mesh
from jax.sharding import PartitionSpec as P

H = 16
AH = 4
QWIN = 32
KWIN = 128
TAIL = (KWIN - QWIN) // 2
HEADROWS = (KWIN + QWIN) // 2
QBLOCK = 128
KBLOCK = QBLOCK + KWIN

norm_eps = 1e-05
masked_value = -1000000000.0
f32 = jnp.float32
bf16 = jnp.bfloat16
NT = (((1,), (1,)), ((), ()))
TOK = ("z", "x", "core")


def sent_around(block, axis, distance):
    size = lax.axis_size(axis)
    return lax.ppermute(block, axis, [(i, (i + distance) % size) for i in range(size)])


def swapped(block, axis, first):
    low = range(first, lax.axis_size(axis) - 1, 2)
    return lax.ppermute(block, axis, [(i, i + 1) for i in low] + [(i + 1, i) for i in low])


def of_everyone(partial):
    return [partial] + [sent_around(partial, "head", d) for d in (1, 2, 3)]


def exchanged(pieces, axis):
    return lax.all_to_all(pieces, axis, split_axis=0, concat_axis=0, tiled=True)


def live_atoms(count_ref):
    live = count_ref[0]
    for i in range(1, count_ref.shape[0]):
        live = live + count_ref[i]
    return live


def layer_norm(value, gain):
    average = jnp.mean(value, axis=-1, keepdims=True)
    centred = value - average
    spread = jnp.mean(centred * centred, axis=-1, keepdims=True)
    return centred * lax.rsqrt(spread + norm_eps) * gain


def halo_kernel(where_ref, count_hbm, atoms_hbm, across, within, counts, atoms, rows, sems):
    copies = [
        pltpu.make_async_copy(count_hbm, counts, sems.at[0]),
        pltpu.make_async_copy(atoms_hbm, atoms, sems.at[1]),
    ]
    for copy in copies:
        copy.start()
    for copy in copies:
        copy.wait()
    live = live_atoms(counts)
    rows[0 : atoms.shape[0]] = atoms[...].astype(f32)
    head_rows = rows[0:HEADROWS]
    tail_rows = rows[pl.ds(live - TAIL, HEADROWS), :]
    even = where_ref[2] == 0
    across[...] = jnp.where(even, head_rows, tail_rows).astype(bf16)
    within[...] = jnp.where(even, tail_rows, head_rows).astype(bf16)


def pair_kernel(pair, w_bias, after, out):
    tokens, keys, channels = pair.shape
    heads = w_bias.shape[0]
    count = 8
    rows = jnp.broadcast_to(w_bias[...].astype(f32)[:, None, :], (heads, count, channels))
    rows = rows.reshape(heads * count, channels)
    query = lax.broadcasted_iota(jnp.int32, rows.shape, 0) % count
    spread = jnp.concatenate(
        [jnp.where(query == q, rows, 0.0).astype(bf16) for q in range(count)], axis=1
    )
    for at in range(0, tokens, count):
        keyed = jnp.concatenate([pair[at + q] for q in range(count)], axis=1)
        terms = lax.dot_general(spread, keyed, NT, preferred_element_type=f32)
        out[:, at : at + count, :] = terms.reshape(heads, count, keys).astype(bf16)


def atom_kernel(
    where_ref, count_ref, counts_row, atoms, across, within, w_atom, w_token, partial, mix, rows
):
    slots = atoms.shape[0]
    tokens = counts_row.shape[1]
    width = w_token.shape[0]
    live = live_atoms(count_ref)
    first = where_ref[0] == 0
    last = where_ref[0] == where_ref[1]
    even = where_ref[2] == 0
    far, near = across[...].astype(f32), within[...].astype(f32)
    rows[0:TAIL] = jnp.where(even, far, near)[:TAIL]
    rows[TAIL : TAIL + slots] = atoms[...].astype(f32)
    rows[TAIL + slots :] = jnp.zeros((HEADROWS, atoms.shape[1]), f32)
    rows[pl.ds(TAIL + live, HEADROWS), :] = jnp.where(even, near, far)
    keyed = rows[...].astype(bf16)

    def weight(part):
        return w_atom[part * width : (part + 1) * width, :]

    queries = lax.dot_general(keyed[TAIL : TAIL + slots], weight(0), NT, preferred_element_type=f32)
    queries = queries.astype(bf16)
    keys = lax.dot_general(keyed, weight(1), NT, preferred_element_type=f32).astype(bf16)
    values = lax.dot_general(weight(2), keyed, NT, preferred_element_type=f32)
    values = jnp.concatenate([values, jnp.ones((16, values.shape[1]), f32)], axis=0).astype(bf16)

    counts = jnp.broadcast_to(counts_row[...].astype(f32), (tokens, tokens))
    token_row = lax.broadcasted_iota(jnp.int32, (tokens, tokens), 0)
    token_lane = lax.broadcasted_iota(jnp.int32, (tokens, tokens), 1)
    starts = jnp.sum(jnp.where(token_lane < token_row, counts, 0.0), axis=1, keepdims=True)
    own = jnp.sum(jnp.where(token_lane == token_row, counts, 0.0), axis=1, keepdims=True)

    row = lax.broadcasted_iota(jnp.int32, (QBLOCK, KBLOCK), 0)
    lane = lax.broadcasted_iota(jnp.int32, (QBLOCK, KBLOCK), 1)
    offset = lane - (row // QWIN) * QWIN
    in_window = jnp.where((offset >= 0) & (offset < KWIN), 0.0, masked_value)
    key_lane = lax.broadcasted_iota(jnp.int32, (1, KBLOCK), 1)
    low = jnp.where(first, 0, -slots)
    high = jnp.where(last, live, 4 * slots)
    query_lane = lax.broadcasted_iota(jnp.int32, (width, QBLOCK), 1)
    slot = lax.broadcasted_iota(jnp.int32, (tokens, QBLOCK), 1).astype(f32)
    totals = jnp.zeros((tokens, width), f32)
    for b in range(slots // QBLOCK):
        at = b * QBLOCK
        key_pos = key_lane + (at - TAIL)
        in_sequence = jnp.where((key_pos >= low) & (key_pos < high), 0.0, masked_value)
        scores = lax.dot_general(
            queries[at : at + QBLOCK], keys[at : at + KBLOCK], NT, preferred_element_type=f32
        ) * width ** (-0.5) + (in_window + in_sequence)
        lifted = jnp.exp(scores - jnp.max(scores, axis=1, keepdims=True)).astype(bf16)
        summed = lax.dot_general(
            values[:, at : at + KBLOCK], lifted, NT, preferred_element_type=f32
        )
        out = jnp.where(query_lane + at < live, summed[:width] / summed[width : width + 1], 0.0)
        out = out.astype(bf16)
        mix[:, at : at + QBLOCK] = out
        member = jnp.where((slot + at >= starts) & (slot + at < starts + own), 1.0, 0.0)
        totals = totals + lax.dot_general(
            member.astype(bf16), out, NT, preferred_element_type=f32
        )
    token_atoms = (totals / own).astype(bf16)
    partial[...] = jnp.dot(token_atoms, w_token[...], preferred_element_type=f32).astype(bf16)


def projection_kernel(p0, p1, p2, p3, single, gain, w_proj, residual, kv, query, gate):
    term = (p0[...].astype(f32) + p1[...].astype(f32)) + (p2[...].astype(f32) + p3[...].astype(f32))
    state = single[...].astype(f32) + term
    residual[...] = state
    normed = layer_norm(state, gain[...].astype(f32)).astype(bf16)
    own = lax.dot_general(normed, w_proj[...], NT, preferred_element_type=f32)
    part = own.shape[1] // 4
    query[...] = own[:, :part].astype(bf16)
    gate[...] = own[:, 3 * part :]
    pair = jnp.concatenate([own[:, 2 * part : 3 * part], own[:, part : 2 * part]], axis=1).astype(bf16)
    for i in range(kv.shape[0]):
        kv[i] = pair


def attention_kernel(
    where_ref, own0, own1, own2, own3, other0, other1, other2, other3, query, gate, bias, w_out,
    partial, kv, scores
):
    core = where_ref[2]
    groups, tokens, width = own0.shape
    for distance, (own, other) in enumerate(
        ((own0, other0), (own1, other1), (own2, other2), (own3, other3))
    ):
        x = (where_ref[4] + 4 - distance) % 4
        kv[:, pl.ds(x, 1), pl.ds(core, 1)] = own[...].reshape(groups, 1, 1, tokens, width)
        kv[:, pl.ds(x, 1), pl.ds(1 - core, 1)] = other[...].reshape(groups, 1, 1, tokens, width)
    part = query.shape[1]
    size = part // 4
    rows = 4 * tokens
    reach = 256
    blank = jnp.zeros((tokens, reach - part), f32)
    spread = jnp.concatenate([blank, query[...].astype(f32)], axis=1)
    spread = jnp.concatenate([spread] * 4, axis=0)
    head = lax.broadcasted_iota(jnp.int32, (rows, reach), 0) // tokens
    lane = lax.broadcasted_iota(jnp.int32, (rows, reach), 1) - (reach - part)
    queries = jnp.where((lane >= head * size) & (lane < (head + 1) * size), spread, 0.0)
    queries = queries.astype(bf16)
    keyed = kv[...].reshape(groups * 8 * tokens, width)
    block = bias.shape[2]
    scale = size ** (-0.5)
    top = None
    for b in range(4):
        s = lax.dot_general(
            queries,
            keyed[b * block : (b + 1) * block, width - reach :],
            NT,
            preferred_element_type=f32,
        ) * scale + bias[4 * b : 4 * b + 4].reshape(rows, block).astype(f32)
        scores[b] = s
        m = jnp.max(s, axis=1, keepdims=True)
        top = m if top is None else jnp.maximum(top, m)
    total = jnp.zeros((rows, 1), f32)
    context = jnp.zeros((rows, part), f32)
    for b in range(4):
        lifted = jnp.exp(scores[b] - top)
        total = total + jnp.sum(lifted, axis=1, keepdims=True)
        context = context + jnp.dot(
            lifted.astype(bf16),
            keyed[b * block : (b + 1) * block, :part],
            preferred_element_type=f32,
        )
    head = lax.broadcasted_iota(jnp.int32, (rows, part), 0) // tokens
    lane = lax.broadcasted_iota(jnp.int32, (rows, part), 1)
    own = (lane >= head * size) & (lane < (head + 1) * size)
    context = jnp.where(own, context / total, 0.0)
    mixed = sum(context[j * tokens : (j + 1) * tokens] for j in range(4))
    gated = (mixed * jax.nn.sigmoid(gate[...])).astype(bf16)
    partial[...] = jnp.dot(gated, w_out[...], preferred_element_type=f32).astype(bf16)


def tail_kernel(
    where_ref, p0, p1, p2, p3, residual, gain, w_trans, w_down, share, update, state
):
    term = (p0[...].astype(f32) + p1[...].astype(f32)) + (p2[...].astype(f32) + p3[...].astype(f32))
    after = residual[...] + term
    quarter = share.shape[1]
    for y in range(4):
        state[y] = after[:, y * quarter : (y + 1) * quarter]
    share[...] = state[where_ref[3]]
    normed = layer_norm(after, gain[...].astype(f32)).astype(bf16)
    gate = jnp.dot(normed, w_trans[0], preferred_element_type=f32)
    up = jnp.dot(normed, w_trans[1], preferred_element_type=f32)
    hidden = (gate * jax.nn.sigmoid(gate) * up).astype(bf16)
    moved = jnp.dot(hidden, w_down[...], preferred_element_type=f32)
    for y in range(4):
        update[y] = moved[:, y * quarter : (y + 1) * quarter].astype(bf16)


def call(kernel, out_shape, operands, scratch, smem):
    vmem = pl.BlockSpec(memory_space=pltpu.VMEM)
    scalar = pl.BlockSpec(memory_space=pltpu.SMEM)
    return pl.pallas_call(
        kernel,
        out_shape=out_shape,
        in_specs=[scalar] * smem + [vmem] * (len(operands) - smem),
        out_specs=jax.tree.map(lambda _: vmem, out_shape),
        scratch_shapes=scratch,
        compiler_params=pltpu.CompilerParams(vmem_limit_bytes=16 << 20),
        cost_estimate=pl.CostEstimate(flops=1 << 30, bytes_accessed=4 << 20, transcendentals=0),
    )(*operands)


def shards(
    single,
    pair,
    atoms,
    atom_counts,
    w_atom,
    w_atom_token,
    ln_gain,
    w_proj,
    w_pair_bias,
    w_out,
    ln_gain2,
    w_trans,
    w_trans_out,
):
    slots, channels = atoms.shape
    tokens, model = single.shape
    where_at = jnp.stack(
        [
            lax.axis_index(TOK),
            jnp.int32(lax.axis_size(TOK) - 1),
            lax.axis_index("core"),
            lax.axis_index("head"),
            lax.axis_index("x"),
        ]
    ).astype(jnp.int32)
    send = jax.ShapeDtypeStruct((HEADROWS, channels), bf16)
    vmem = pl.BlockSpec(memory_space=pltpu.VMEM)
    hbm = pl.BlockSpec(memory_space=pl.ANY)
    sent_across, sent_within = pl.pallas_call(
        halo_kernel,
        out_shape=(send, send),
        in_specs=[pl.BlockSpec(memory_space=pltpu.SMEM), hbm, hbm],
        out_specs=(vmem, vmem),
        scratch_shapes=[
            pltpu.SMEM((tokens,), jnp.int32),
            pltpu.VMEM((slots, channels), bf16),
            pltpu.VMEM((slots + HEADROWS, channels), f32),
            pltpu.SemaphoreType.DMA((2,)),
        ],
        compiler_params=pltpu.CompilerParams(vmem_limit_bytes=4 << 20),
        cost_estimate=pl.CostEstimate(flops=1 << 33, bytes_accessed=32 << 20, transcendentals=0),
    )(
        where_at,
        pltpu.with_memory_space_constraint(atom_counts, pltpu.HBM),
        pltpu.with_memory_space_constraint(atoms, pltpu.HBM),
    )
    across = swapped(sent_across, TOK, 1)
    within = swapped(sent_within, TOK, 0)
    keys = pair.shape[1]
    pair_term = pl.pallas_call(
        pair_kernel,
        out_shape=jax.ShapeDtypeStruct((H, tokens, keys), bf16),
        in_specs=[vmem, vmem, hbm],
        out_specs=vmem,
        compiler_params=pltpu.CompilerParams(vmem_limit_bytes=16 << 20),
        cost_estimate=pl.CostEstimate(flops=2 << 30, bytes_accessed=8 << 20, transcendentals=0),
    )(pair, w_pair_bias.T, sent_across)
    pair_term, across, within = lax.optimization_barrier((pair_term, across, within))
    bias = exchanged(pair_term, "head")

    width = w_atom.shape[2]
    partial, mix = call(
        atom_kernel,
        (
            jax.ShapeDtypeStruct((tokens, model), bf16),
            jax.ShapeDtypeStruct((width, slots), bf16),
        ),
        (
            where_at,
            atom_counts,
            atom_counts.reshape(1, tokens),
            atoms,
            across,
            within,
            w_atom.transpose(1, 2, 0).reshape(3 * width, channels),
            w_atom_token,
        ),
        [pltpu.VMEM((TAIL + slots + HEADROWS, channels), f32)],
        2,
    )
    quarter = model // 4
    residual, kv, query, gate = call(
        projection_kernel,
        (
            jax.ShapeDtypeStruct((tokens, model), f32),
            jax.ShapeDtypeStruct((8, tokens, 2 * quarter), bf16),
            jax.ShapeDtypeStruct((tokens, quarter), bf16),
            jax.ShapeDtypeStruct((tokens, quarter), f32),
        ),
        (
            *of_everyone(partial),
            single,
            ln_gain.reshape(1, model),
            w_proj.transpose(1, 2, 0).reshape(-1, model),
        ),
        [],
        0,
    )
    kv, bias = lax.optimization_barrier((kv, bias))
    kv_own = exchanged(kv, "z")
    kv_own = [kv_own] + [sent_around(kv_own, "x", d) for d in (1, 2, 3)]
    kv_other = [sent_around(piece, "core", 1) for piece in kv_own]
    partial = call(
        attention_kernel,
        jax.ShapeDtypeStruct((tokens, model), bf16),
        (where_at, *kv_own, *kv_other, query, gate, bias, w_out),
        [
            pltpu.VMEM((8, 4, 2, tokens, 2 * quarter), bf16),
            pltpu.VMEM((4, 4 * tokens, bias.shape[2]), f32),
        ],
        1,
    )
    share, update = call(
        tail_kernel,
        (
            jax.ShapeDtypeStruct((tokens, quarter), f32),
            jax.ShapeDtypeStruct((4, tokens, quarter), bf16),
        ),
        (
            where_at,
            *of_everyone(partial),
            residual,
            ln_gain2.reshape(1, model),
            w_trans.transpose(1, 0, 2),
            w_trans_out,
        ),
        [pltpu.VMEM((4, tokens, quarter), f32)],
        1,
    )
    update = exchanged(update, "head")
    refined = (share + update.astype(f32).sum(axis=0)).astype(bf16)
    return (refined, mix)


def solution(mesh):
    devices = mesh.devices.reshape(8, 4, 2, 4)
    return jax.shard_map(
        shards,
        mesh=Mesh(devices, ("z", "x", "core", "head")),
        in_specs=(
            P(TOK, None),
            P(TOK, "head", None),
            P(TOK, None),
            P(TOK),
            P(None, None, "head"),
            P("head", None),
            P(),
            P(None, None, "head"),
            P(),
            P("head", None),
            P(),
            P(None, None, "head"),
            P("head", None),
        ),
        out_specs=(P(TOK, "head"), P("head", TOK)),
        check_vma=False,
    )
```

```python
import jax
import jax.numpy as jnp
from jax import lax
from jax.experimental import pallas as pl
from jax.experimental.pallas import tpu as pltpu
from jax.sharding import Mesh
from jax.sharding import PartitionSpec as P

H = 16
AH = 4
QWIN = 32
KWIN = 128
TAIL = (KWIN - QWIN) // 2
HEADROWS = (KWIN + QWIN) // 2
QBLOCK = 128
KBLOCK = QBLOCK + KWIN

norm_eps = 1e-05
masked_value = -1000000000.0
f32 = jnp.float32
bf16 = jnp.bfloat16
NT = (((1,), (1,)), ((), ()))
TOK = ("z", "x", "core")


def sent_around(block, axis, distance):
    size = lax.axis_size(axis)
    return lax.ppermute(block, axis, [(i, (i + distance) % size) for i in range(size)])


def swapped(block, axis, first):
    low = range(first, lax.axis_size(axis) - 1, 2)
    return lax.ppermute(block, axis, [(i, i + 1) for i in low] + [(i + 1, i) for i in low])


def of_everyone(partial):
    return [partial] + [sent_around(partial, "head", d) for d in (1, 2, 3)]


def exchanged(pieces, axis):
    return lax.all_to_all(pieces, axis, split_axis=0, concat_axis=0, tiled=True)


def live_atoms(count_ref):
    live = count_ref[0]
    for i in range(1, count_ref.shape[0]):
        live = live + count_ref[i]
    return live


def layer_norm(value, gain):
    average = jnp.mean(value, axis=-1, keepdims=True)
    centred = value - average
    spread = jnp.mean(centred * centred, axis=-1, keepdims=True)
    return centred * lax.rsqrt(spread + norm_eps) * gain


def halo_kernel(where_ref, count_hbm, atoms_hbm, across, within, counts, atoms, rows, sems):
    copies = [
        pltpu.make_async_copy(count_hbm, counts, sems.at[0]),
        pltpu.make_async_copy(atoms_hbm, atoms, sems.at[1]),
    ]
    for copy in copies:
        copy.start()
    for copy in copies:
        copy.wait()
    live = live_atoms(counts)
    rows[0 : atoms.shape[0]] = atoms[...].astype(f32)
    head_rows = rows[0:HEADROWS]
    tail_rows = rows[pl.ds(live - TAIL, HEADROWS), :]
    even = where_ref[2] == 0
    across[...] = jnp.where(even, head_rows, tail_rows).astype(bf16)
    within[...] = jnp.where(even, tail_rows, head_rows).astype(bf16)


def pair_kernel(where_ref, pair, w_bias, after, out0, out1, out2, out3, out):
    tokens, keys, channels = pair.shape
    heads = w_bias.shape[0]
    count = 8
    rows = jnp.broadcast_to(w_bias[...].astype(f32)[:, None, :], (heads, count, channels))
    rows = rows.reshape(heads * count, channels)
    query = lax.broadcasted_iota(jnp.int32, rows.shape, 0) % count
    spread = jnp.concatenate(
        [jnp.where(query == q, rows, 0.0).astype(bf16) for q in range(count)], axis=1
    )
    for at in range(0, tokens, count):
        keyed = jnp.concatenate([pair[at + q] for q in range(count)], axis=1)
        terms = lax.dot_general(spread, keyed, NT, preferred_element_type=f32)
        out[:, at : at + count, :] = terms.reshape(heads, count, keys).astype(bf16)
    for distance, piece in enumerate((out0, out1, out2, out3)):
        piece[...] = out[pl.ds(4 * ((where_ref[3] + distance) % 4), 4)]


def atom_kernel(
    where_ref, count_ref, counts_row, atoms, across, within, w_atom, w_token, partial, mix, rows
):
    slots = atoms.shape[0]
    tokens = counts_row.shape[1]
    width = w_token.shape[0]
    live = live_atoms(count_ref)
    first = where_ref[0] == 0
    last = where_ref[0] == where_ref[1]
    even = where_ref[2] == 0
    far, near = across[...].astype(f32), within[...].astype(f32)
    rows[0:TAIL] = jnp.where(even, far, near)[:TAIL]
    rows[TAIL : TAIL + slots] = atoms[...].astype(f32)
    rows[TAIL + slots :] = jnp.zeros((HEADROWS, atoms.shape[1]), f32)
    rows[pl.ds(TAIL + live, HEADROWS), :] = jnp.where(even, near, far)
    keyed = rows[...].astype(bf16)

    def weight(part):
        return w_atom[part * width : (part + 1) * width, :]

    queries = lax.dot_general(keyed[TAIL : TAIL + slots], weight(0), NT, preferred_element_type=f32)
    queries = queries.astype(bf16)
    keys = lax.dot_general(keyed, weight(1), NT, preferred_element_type=f32).astype(bf16)
    values = lax.dot_general(weight(2), keyed, NT, preferred_element_type=f32)
    values = jnp.concatenate([values, jnp.ones((16, values.shape[1]), f32)], axis=0).astype(bf16)

    counts = jnp.broadcast_to(counts_row[...].astype(f32), (tokens, tokens))
    token_row = lax.broadcasted_iota(jnp.int32, (tokens, tokens), 0)
    token_lane = lax.broadcasted_iota(jnp.int32, (tokens, tokens), 1)
    starts = jnp.sum(jnp.where(token_lane < token_row, counts, 0.0), axis=1, keepdims=True)
    own = jnp.sum(jnp.where(token_lane == token_row, counts, 0.0), axis=1, keepdims=True)

    row = lax.broadcasted_iota(jnp.int32, (QBLOCK, KBLOCK), 0)
    lane = lax.broadcasted_iota(jnp.int32, (QBLOCK, KBLOCK), 1)
    offset = lane - (row // QWIN) * QWIN
    in_window = jnp.where((offset >= 0) & (offset < KWIN), 0.0, masked_value)
    key_lane = lax.broadcasted_iota(jnp.int32, (1, KBLOCK), 1)
    low = jnp.where(first, 0, -slots)
    high = jnp.where(last, live, 4 * slots)
    query_lane = lax.broadcasted_iota(jnp.int32, (width, QBLOCK), 1)
    slot = lax.broadcasted_iota(jnp.int32, (tokens, QBLOCK), 1).astype(f32)
    totals = jnp.zeros((tokens, width), f32)
    for b in range(slots // QBLOCK):
        at = b * QBLOCK
        key_pos = key_lane + (at - TAIL)
        in_sequence = jnp.where((key_pos >= low) & (key_pos < high), 0.0, masked_value)
        scores = lax.dot_general(
            queries[at : at + QBLOCK], keys[at : at + KBLOCK], NT, preferred_element_type=f32
        ) * width ** (-0.5) + (in_window + in_sequence)
        lifted = jnp.exp(scores - jnp.max(scores, axis=1, keepdims=True)).astype(bf16)
        summed = lax.dot_general(
            values[:, at : at + KBLOCK], lifted, NT, preferred_element_type=f32
        )
        out = jnp.where(query_lane + at < live, summed[:width] / summed[width : width + 1], 0.0)
        out = out.astype(bf16)
        mix[:, at : at + QBLOCK] = out
        member = jnp.where((slot + at >= starts) & (slot + at < starts + own), 1.0, 0.0)
        totals = totals + lax.dot_general(
            member.astype(bf16), out, NT, preferred_element_type=f32
        )
    token_atoms = (totals / own).astype(bf16)
    partial[...] = jnp.dot(token_atoms, w_token[...], preferred_element_type=f32).astype(bf16)


def projection_kernel(p0, p1, p2, p3, single, gain, w_proj, residual, kv, query, gate):
    term = (p0[...].astype(f32) + p1[...].astype(f32)) + (p2[...].astype(f32) + p3[...].astype(f32))
    state = single[...].astype(f32) + term
    residual[...] = state
    normed = layer_norm(state, gain[...].astype(f32)).astype(bf16)
    own = lax.dot_general(normed, w_proj[...], NT, preferred_element_type=f32)
    part = own.shape[1] // 4
    query[...] = own[:, :part].astype(bf16)
    gate[...] = own[:, 3 * part :]
    pair = jnp.concatenate([own[:, 2 * part : 3 * part], own[:, part : 2 * part]], axis=1).astype(bf16)
    for i in range(kv.shape[0]):
        kv[i] = pair


def attention_kernel(
    where_ref, own0, own1, own2, own3, other0, other1, other2, other3, query, gate,
    bias0, bias1, bias2, bias3, w_out, partial, kv, scores
):
    core = where_ref[2]
    groups, tokens, width = own0.shape
    for distance, (own, other) in enumerate(
        ((own0, other0), (own1, other1), (own2, other2), (own3, other3))
    ):
        x = (where_ref[4] + 4 - distance) % 4
        kv[:, pl.ds(x, 1), pl.ds(core, 1)] = own[...].reshape(groups, 1, 1, tokens, width)
        kv[:, pl.ds(x, 1), pl.ds(1 - core, 1)] = other[...].reshape(groups, 1, 1, tokens, width)
    part = query.shape[1]
    size = part // 4
    rows = 4 * tokens
    reach = 256
    blank = jnp.zeros((tokens, reach - part), f32)
    spread = jnp.concatenate([blank, query[...].astype(f32)], axis=1)
    spread = jnp.concatenate([spread] * 4, axis=0)
    head = lax.broadcasted_iota(jnp.int32, (rows, reach), 0) // tokens
    lane = lax.broadcasted_iota(jnp.int32, (rows, reach), 1) - (reach - part)
    queries = jnp.where((lane >= head * size) & (lane < (head + 1) * size), spread, 0.0)
    queries = queries.astype(bf16)
    block = bias0.shape[2]
    scale = size ** (-0.5)
    top = None
    for b, bias in enumerate((bias0, bias1, bias2, bias3)):
        keyed = kv[pl.ds(2 * ((where_ref[3] + 4 - b) % 4), 2)].reshape(block, width)
        s = lax.dot_general(
            queries, keyed[:, width - reach :], NT, preferred_element_type=f32
        ) * scale + bias[...].reshape(rows, block).astype(f32)
        scores[b] = s
        m = jnp.max(s, axis=1, keepdims=True)
        top = m if top is None else jnp.maximum(top, m)
    total = jnp.zeros((rows, 1), f32)
    context = jnp.zeros((rows, part), f32)
    for b in range(4):
        lifted = jnp.exp(scores[b] - top)
        total = total + jnp.sum(lifted, axis=1, keepdims=True)
        keyed = kv[pl.ds(2 * ((where_ref[3] + 4 - b) % 4), 2)].reshape(block, width)
        context = context + jnp.dot(
            lifted.astype(bf16), keyed[:, :part], preferred_element_type=f32
        )
    head = lax.broadcasted_iota(jnp.int32, (rows, part), 0) // tokens
    lane = lax.broadcasted_iota(jnp.int32, (rows, part), 1)
    own = (lane >= head * size) & (lane < (head + 1) * size)
    context = jnp.where(own, context / total, 0.0)
    mixed = sum(context[j * tokens : (j + 1) * tokens] for j in range(4))
    gated = (mixed * jax.nn.sigmoid(gate[...])).astype(bf16)
    partial[...] = jnp.dot(gated, w_out[...], preferred_element_type=f32).astype(bf16)


def tail_kernel(
    where_ref, p0, p1, p2, p3, residual, gain, w_trans, w_down, share, update, state
):
    term = (p0[...].astype(f32) + p1[...].astype(f32)) + (p2[...].astype(f32) + p3[...].astype(f32))
    after = residual[...] + term
    quarter = share.shape[1]
    for y in range(4):
        state[y] = after[:, y * quarter : (y + 1) * quarter]
    share[...] = state[where_ref[3]]
    normed = layer_norm(after, gain[...].astype(f32)).astype(bf16)
    gate = jnp.dot(normed, w_trans[0], preferred_element_type=f32)
    up = jnp.dot(normed, w_trans[1], preferred_element_type=f32)
    hidden = (gate * jax.nn.sigmoid(gate) * up).astype(bf16)
    moved = jnp.dot(hidden, w_down[...], preferred_element_type=f32)
    for y in range(4):
        update[y] = moved[:, y * quarter : (y + 1) * quarter].astype(bf16)


def call(kernel, out_shape, operands, scratch, smem):
    vmem = pl.BlockSpec(memory_space=pltpu.VMEM)
    scalar = pl.BlockSpec(memory_space=pltpu.SMEM)
    return pl.pallas_call(
        kernel,
        out_shape=out_shape,
        in_specs=[scalar] * smem + [vmem] * (len(operands) - smem),
        out_specs=jax.tree.map(lambda _: vmem, out_shape),
        scratch_shapes=scratch,
        compiler_params=pltpu.CompilerParams(vmem_limit_bytes=16 << 20),
        cost_estimate=pl.CostEstimate(flops=1 << 30, bytes_accessed=4 << 20, transcendentals=0),
    )(*operands)


def shards(
    single,
    pair,
    atoms,
    atom_counts,
    w_atom,
    w_atom_token,
    ln_gain,
    w_proj,
    w_pair_bias,
    w_out,
    ln_gain2,
    w_trans,
    w_trans_out,
):
    slots, channels = atoms.shape
    tokens, model = single.shape
    where_at = jnp.stack(
        [
            lax.axis_index(TOK),
            jnp.int32(lax.axis_size(TOK) - 1),
            lax.axis_index("core"),
            lax.axis_index("head"),
            lax.axis_index("x"),
        ]
    ).astype(jnp.int32)
    send = jax.ShapeDtypeStruct((HEADROWS, channels), bf16)
    vmem = pl.BlockSpec(memory_space=pltpu.VMEM)
    hbm = pl.BlockSpec(memory_space=pl.ANY)
    sent_across, sent_within = pl.pallas_call(
        halo_kernel,
        out_shape=(send, send),
        in_specs=[pl.BlockSpec(memory_space=pltpu.SMEM), hbm, hbm],
        out_specs=(vmem, vmem),
        scratch_shapes=[
            pltpu.SMEM((tokens,), jnp.int32),
            pltpu.VMEM((slots, channels), bf16),
            pltpu.VMEM((slots + HEADROWS, channels), f32),
            pltpu.SemaphoreType.DMA((2,)),
        ],
        compiler_params=pltpu.CompilerParams(vmem_limit_bytes=4 << 20),
        cost_estimate=pl.CostEstimate(flops=1 << 33, bytes_accessed=32 << 20, transcendentals=0),
    )(
        where_at,
        pltpu.with_memory_space_constraint(atom_counts, pltpu.HBM),
        pltpu.with_memory_space_constraint(atoms, pltpu.HBM),
    )
    across = swapped(sent_across, TOK, 1)
    within = swapped(sent_within, TOK, 0)
    keys = pair.shape[1]
    piece = jax.ShapeDtypeStruct((4, tokens, keys), bf16)
    bias = pl.pallas_call(
        pair_kernel,
        out_shape=(piece, piece, piece, piece),
        in_specs=[pl.BlockSpec(memory_space=pltpu.SMEM), vmem, vmem, hbm],
        out_specs=(vmem, vmem, vmem, vmem),
        scratch_shapes=[pltpu.VMEM((H, tokens, keys), bf16)],
        compiler_params=pltpu.CompilerParams(vmem_limit_bytes=16 << 20),
        cost_estimate=pl.CostEstimate(flops=2 << 30, bytes_accessed=8 << 20, transcendentals=0),
    )(where_at, pair, w_pair_bias.T, sent_across)
    across, within, *bias = lax.optimization_barrier((across, within, *bias))

    width = w_atom.shape[2]
    partial, mix = call(
        atom_kernel,
        (
            jax.ShapeDtypeStruct((tokens, model), bf16),
            jax.ShapeDtypeStruct((width, slots), bf16),
        ),
        (
            where_at,
            atom_counts,
            atom_counts.reshape(1, tokens),
            atoms,
            across,
            within,
            w_atom.transpose(1, 2, 0).reshape(3 * width, channels),
            w_atom_token,
        ),
        [pltpu.VMEM((TAIL + slots + HEADROWS, channels), f32)],
        2,
    )
    quarter = model // 4
    partials = of_everyone(partial)
    partial, *bias = lax.optimization_barrier((partial, *bias))
    bias = [bias[0]] + [sent_around(bias[d], "head", d) for d in (1, 2, 3)]
    residual, kv, query, gate = call(
        projection_kernel,
        (
            jax.ShapeDtypeStruct((tokens, model), f32),
            jax.ShapeDtypeStruct((8, tokens, 2 * quarter), bf16),
            jax.ShapeDtypeStruct((tokens, quarter), bf16),
            jax.ShapeDtypeStruct((tokens, quarter), f32),
        ),
        (
            *partials,
            single,
            ln_gain.reshape(1, model),
            w_proj.transpose(1, 2, 0).reshape(-1, model),
        ),
        [],
        0,
    )
    kv_own = exchanged(kv, "z")
    kv_own, *bias = lax.optimization_barrier((kv_own, *bias))
    kv_own = [kv_own] + [sent_around(kv_own, "x", d) for d in (1, 2, 3)]
    kv_other = [sent_around(piece, "core", 1) for piece in kv_own]
    partial = call(
        attention_kernel,
        jax.ShapeDtypeStruct((tokens, model), bf16),
        (where_at, *kv_own, *kv_other, query, gate, *bias, w_out),
        [
            pltpu.VMEM((8, 4, 2, tokens, 2 * quarter), bf16),
            pltpu.VMEM((4, 4 * tokens, keys), f32),
        ],
        1,
    )
    share, update = call(
        tail_kernel,
        (
            jax.ShapeDtypeStruct((tokens, quarter), f32),
            jax.ShapeDtypeStruct((4, tokens, quarter), bf16),
        ),
        (
            where_at,
            *of_everyone(partial),
            residual,
            ln_gain2.reshape(1, model),
            w_trans.transpose(1, 0, 2),
            w_trans_out,
        ),
        [pltpu.VMEM((4, tokens, quarter), f32)],
        1,
    )
    update = exchanged(update, "head")
    refined = (share + update.astype(f32).sum(axis=0)).astype(bf16)
    return (refined, mix)


def solution(mesh):
    devices = mesh.devices.reshape(8, 4, 2, 4)
    return jax.shard_map(
        shards,
        mesh=Mesh(devices, ("z", "x", "core", "head")),
        in_specs=(
            P(TOK, None),
            P(TOK, "head", None),
            P(TOK, None),
            P(TOK),
            P(None, None, "head"),
            P("head", None),
            P(),
            P(None, None, "head"),
            P(),
            P("head", None),
            P(),
            P(None, None, "head"),
            P("head", None),
        ),
        out_specs=(P(TOK, "head"), P("head", TOK)),
        check_vma=False,
    )
```

```python
import jax
import jax.numpy as jnp
from jax import lax
from jax.experimental import pallas as pl
from jax.experimental.pallas import tpu as pltpu
from jax.sharding import Mesh
from jax.sharding import PartitionSpec as P

H = 16
AH = 4
QWIN = 32
KWIN = 128
TAIL = (KWIN - QWIN) // 2
HEADROWS = (KWIN + QWIN) // 2
QBLOCK = 128
KBLOCK = QBLOCK + KWIN

norm_eps = 1e-05
masked_value = -1000000000.0
f32 = jnp.float32
bf16 = jnp.bfloat16
NT = (((1,), (1,)), ((), ()))
TOK = ("z", "x", "core")


def sent_around(block, axis, distance):
    size = lax.axis_size(axis)
    return lax.ppermute(block, axis, [(i, (i + distance) % size) for i in range(size)])


def swapped(block, axis, first):
    low = range(first, lax.axis_size(axis) - 1, 2)
    return lax.ppermute(block, axis, [(i, i + 1) for i in low] + [(i + 1, i) for i in low])


def of_everyone(partial):
    return [partial] + [sent_around(partial, "head", d) for d in (1, 2, 3)]


def exchanged(pieces, axis):
    return lax.all_to_all(pieces, axis, split_axis=0, concat_axis=0, tiled=True)


def live_atoms(count_ref):
    live = count_ref[0]
    for i in range(1, count_ref.shape[0]):
        live = live + count_ref[i]
    return live


def layer_norm(value, gain):
    average = jnp.mean(value, axis=-1, keepdims=True)
    centred = value - average
    spread = jnp.mean(centred * centred, axis=-1, keepdims=True)
    return centred * lax.rsqrt(spread + norm_eps) * gain


def halo_kernel(where_ref, count_hbm, atoms_hbm, across, within, counts, atoms, rows, sems):
    copies = [
        pltpu.make_async_copy(count_hbm, counts, sems.at[0]),
        pltpu.make_async_copy(atoms_hbm, atoms, sems.at[1]),
    ]
    for copy in copies:
        copy.start()
    for copy in copies:
        copy.wait()
    live = live_atoms(counts)
    rows[0 : atoms.shape[0]] = atoms[...].astype(f32)
    head_rows = rows[0:HEADROWS]
    tail_rows = rows[pl.ds(live - TAIL, HEADROWS), :]
    even = where_ref[2] == 0
    across[...] = jnp.where(even, head_rows, tail_rows).astype(bf16)
    within[...] = jnp.where(even, tail_rows, head_rows).astype(bf16)


def pair_kernel(where_ref, pair, w_bias, after, out0, out1, out2, out3, out):
    tokens, keys, channels = pair.shape
    heads = w_bias.shape[0]
    count = 8
    rows = jnp.broadcast_to(w_bias[...].astype(f32)[:, None, :], (heads, count, channels))
    rows = rows.reshape(heads * count, channels)
    query = lax.broadcasted_iota(jnp.int32, rows.shape, 0) % count
    spread = jnp.concatenate(
        [jnp.where(query == q, rows, 0.0).astype(bf16) for q in range(count)], axis=1
    )
    for at in range(0, tokens, count):
        keyed = jnp.concatenate([pair[at + q] for q in range(count)], axis=1)
        terms = lax.dot_general(spread, keyed, NT, preferred_element_type=f32)
        out[:, at : at + count, :] = terms.reshape(heads, count, keys).astype(bf16)
    for distance, piece in enumerate((out0, out1, out2, out3)):
        piece[...] = out[pl.ds(4 * ((where_ref[3] + distance) % 4), 4)]


def atom_kernel(
    where_ref, count_ref, counts_row, atoms, across, within, w_atom, w_token, partial, mix, rows
):
    slots = atoms.shape[0]
    tokens = counts_row.shape[1]
    width = w_token.shape[0]
    live = live_atoms(count_ref)
    first = where_ref[0] == 0
    last = where_ref[0] == where_ref[1]
    even = where_ref[2] == 0
    far, near = across[...].astype(f32), within[...].astype(f32)
    rows[0:TAIL] = jnp.where(even, far, near)[:TAIL]
    rows[TAIL : TAIL + slots] = atoms[...].astype(f32)
    rows[TAIL + slots :] = jnp.zeros((HEADROWS, atoms.shape[1]), f32)
    rows[pl.ds(TAIL + live, HEADROWS), :] = jnp.where(even, near, far)
    keyed = rows[...].astype(bf16)

    def weight(part):
        return w_atom[part * width : (part + 1) * width, :]

    queries = lax.dot_general(keyed[TAIL : TAIL + slots], weight(0), NT, preferred_element_type=f32)
    queries = queries.astype(bf16)
    keys = lax.dot_general(keyed, weight(1), NT, preferred_element_type=f32).astype(bf16)
    values = lax.dot_general(weight(2), keyed, NT, preferred_element_type=f32)
    values = jnp.concatenate([values, jnp.ones((16, values.shape[1]), f32)], axis=0).astype(bf16)

    counts = jnp.broadcast_to(counts_row[...].astype(f32), (tokens, tokens))
    token_row = lax.broadcasted_iota(jnp.int32, (tokens, tokens), 0)
    token_lane = lax.broadcasted_iota(jnp.int32, (tokens, tokens), 1)
    starts = jnp.sum(jnp.where(token_lane < token_row, counts, 0.0), axis=1, keepdims=True)
    own = jnp.sum(jnp.where(token_lane == token_row, counts, 0.0), axis=1, keepdims=True)

    row = lax.broadcasted_iota(jnp.int32, (QBLOCK, KBLOCK), 0)
    lane = lax.broadcasted_iota(jnp.int32, (QBLOCK, KBLOCK), 1)
    offset = lane - (row // QWIN) * QWIN
    in_window = jnp.where((offset >= 0) & (offset < KWIN), 0.0, masked_value)
    key_lane = lax.broadcasted_iota(jnp.int32, (1, KBLOCK), 1)
    low = jnp.where(first, 0, -slots)
    high = jnp.where(last, live, 4 * slots)
    query_lane = lax.broadcasted_iota(jnp.int32, (width, QBLOCK), 1)
    slot = lax.broadcasted_iota(jnp.int32, (tokens, QBLOCK), 1).astype(f32)
    totals = jnp.zeros((tokens, width), f32)
    for b in range(slots // QBLOCK):
        at = b * QBLOCK
        key_pos = key_lane + (at - TAIL)
        in_sequence = jnp.where((key_pos >= low) & (key_pos < high), 0.0, masked_value)
        scores = lax.dot_general(
            queries[at : at + QBLOCK], keys[at : at + KBLOCK], NT, preferred_element_type=f32
        ) * width ** (-0.5) + (in_window + in_sequence)
        lifted = jnp.exp(scores - jnp.max(scores, axis=1, keepdims=True)).astype(bf16)
        summed = lax.dot_general(
            values[:, at : at + KBLOCK], lifted, NT, preferred_element_type=f32
        )
        out = jnp.where(query_lane + at < live, summed[:width] / summed[width : width + 1], 0.0)
        out = out.astype(bf16)
        mix[:, at : at + QBLOCK] = out
        member = jnp.where((slot + at >= starts) & (slot + at < starts + own), 1.0, 0.0)
        totals = totals + lax.dot_general(
            member.astype(bf16), out, NT, preferred_element_type=f32
        )
    token_atoms = (totals / own).astype(bf16)
    partial[...] = jnp.dot(token_atoms, w_token[...], preferred_element_type=f32).astype(bf16)


def projection_kernel(p0, p1, p2, p3, single, gain, w_proj, residual, kv, query, gate):
    term = (p0[...].astype(f32) + p1[...].astype(f32)) + (p2[...].astype(f32) + p3[...].astype(f32))
    state = single[...].astype(f32) + term
    residual[...] = state
    normed = layer_norm(state, gain[...].astype(f32)).astype(bf16)
    own = lax.dot_general(normed, w_proj[...], NT, preferred_element_type=f32)
    part = own.shape[1] // 4
    query[...] = own[:, :part].astype(bf16)
    gate[...] = own[:, 3 * part :]
    pair = jnp.concatenate([own[:, 2 * part : 3 * part], own[:, part : 2 * part]], axis=1).astype(bf16)
    for i in range(kv.shape[0]):
        kv[i] = pair


def attention_kernel(
    where_ref, own0, own1, own2, own3, other0, other1, other2, other3, query, gate,
    bias0, bias1, bias2, bias3, w_out, partial, kv, scores
):
    core = where_ref[2]
    groups, tokens, width = own0.shape
    for distance, (own, other) in enumerate(
        ((own0, other0), (own1, other1), (own2, other2), (own3, other3))
    ):
        x = (where_ref[4] + 4 - distance) % 4
        kv[:, pl.ds(x, 1), pl.ds(core, 1)] = own[...].reshape(groups, 1, 1, tokens, width)
        kv[:, pl.ds(x, 1), pl.ds(1 - core, 1)] = other[...].reshape(groups, 1, 1, tokens, width)
    part = query.shape[1]
    size = part // 4
    rows = 4 * tokens
    reach = 256
    blank = jnp.zeros((tokens, reach - part), f32)
    spread = jnp.concatenate([blank, query[...].astype(f32)], axis=1)
    spread = jnp.concatenate([spread] * 4, axis=0)
    head = lax.broadcasted_iota(jnp.int32, (rows, reach), 0) // tokens
    lane = lax.broadcasted_iota(jnp.int32, (rows, reach), 1) - (reach - part)
    queries = jnp.where((lane >= head * size) & (lane < (head + 1) * size), spread, 0.0)
    queries = queries.astype(bf16)
    block = bias0.shape[2]
    scale = size ** (-0.5)
    top = None
    for b, bias in enumerate((bias0, bias1, bias2, bias3)):
        keyed = kv[pl.ds(2 * ((where_ref[3] + 4 - b) % 4), 2)].reshape(block, width)
        s = lax.dot_general(
            queries, keyed[:, width - reach :], NT, preferred_element_type=f32
        ) * scale + bias[...].reshape(rows, block).astype(f32)
        scores[b] = s
        m = jnp.max(s, axis=1, keepdims=True)
        top = m if top is None else jnp.maximum(top, m)
    total = jnp.zeros((rows, 1), f32)
    context = jnp.zeros((rows, part), f32)
    for b in range(4):
        lifted = jnp.exp(scores[b] - top)
        total = total + jnp.sum(lifted, axis=1, keepdims=True)
        keyed = kv[pl.ds(2 * ((where_ref[3] + 4 - b) % 4), 2)].reshape(block, width)
        context = context + jnp.dot(
            lifted.astype(bf16), keyed[:, :part], preferred_element_type=f32
        )
    head = lax.broadcasted_iota(jnp.int32, (rows, part), 0) // tokens
    lane = lax.broadcasted_iota(jnp.int32, (rows, part), 1)
    own = (lane >= head * size) & (lane < (head + 1) * size)
    context = jnp.where(own, context / total, 0.0)
    mixed = sum(context[j * tokens : (j + 1) * tokens] for j in range(4))
    gated = (mixed * jax.nn.sigmoid(gate[...])).astype(bf16)
    partial[...] = jnp.dot(gated, w_out[...], preferred_element_type=f32).astype(bf16)


def tail_kernel(
    where_ref, p0, p1, p2, p3, residual, gain, w_trans, w_down, share, update1, update2, update3, state,
    moved_rows
):
    term = (p0[...].astype(f32) + p1[...].astype(f32)) + (p2[...].astype(f32) + p3[...].astype(f32))
    after = residual[...] + term
    quarter = share.shape[1]
    for y in range(4):
        state[y] = after[:, y * quarter : (y + 1) * quarter]
    normed = layer_norm(after, gain[...].astype(f32)).astype(bf16)
    gate = jnp.dot(normed, w_trans[0], preferred_element_type=f32)
    up = jnp.dot(normed, w_trans[1], preferred_element_type=f32)
    hidden = (gate * jax.nn.sigmoid(gate) * up).astype(bf16)
    moved = jnp.dot(hidden, w_down[...], preferred_element_type=f32)
    for y in range(4):
        moved_rows[y] = moved[:, y * quarter : (y + 1) * quarter]
    head = where_ref[3]
    share[...] = state[head] + moved_rows[head]
    for distance, update in ((1, update1), (2, update2), (3, update3)):
        update[...] = moved_rows[(head + distance) % 4].astype(bf16)


def call(kernel, out_shape, operands, scratch, smem):
    vmem = pl.BlockSpec(memory_space=pltpu.VMEM)
    scalar = pl.BlockSpec(memory_space=pltpu.SMEM)
    return pl.pallas_call(
        kernel,
        out_shape=out_shape,
        in_specs=[scalar] * smem + [vmem] * (len(operands) - smem),
        out_specs=jax.tree.map(lambda _: vmem, out_shape),
        scratch_shapes=scratch,
        compiler_params=pltpu.CompilerParams(vmem_limit_bytes=16 << 20),
        cost_estimate=pl.CostEstimate(flops=1 << 30, bytes_accessed=4 << 20, transcendentals=0),
    )(*operands)


def shards(
    single,
    pair,
    atoms,
    atom_counts,
    w_atom,
    w_atom_token,
    ln_gain,
    w_proj,
    w_pair_bias,
    w_out,
    ln_gain2,
    w_trans,
    w_trans_out,
):
    slots, channels = atoms.shape
    tokens, model = single.shape
    where_at = jnp.stack(
        [
            lax.axis_index(TOK),
            jnp.int32(lax.axis_size(TOK) - 1),
            lax.axis_index("core"),
            lax.axis_index("head"),
            lax.axis_index("x"),
        ]
    ).astype(jnp.int32)
    send = jax.ShapeDtypeStruct((HEADROWS, channels), bf16)
    vmem = pl.BlockSpec(memory_space=pltpu.VMEM)
    hbm = pl.BlockSpec(memory_space=pl.ANY)
    sent_across, sent_within = pl.pallas_call(
        halo_kernel,
        out_shape=(send, send),
        in_specs=[pl.BlockSpec(memory_space=pltpu.SMEM), hbm, hbm],
        out_specs=(vmem, vmem),
        scratch_shapes=[
            pltpu.SMEM((tokens,), jnp.int32),
            pltpu.VMEM((slots, channels), bf16),
            pltpu.VMEM((slots + HEADROWS, channels), f32),
            pltpu.SemaphoreType.DMA((2,)),
        ],
        compiler_params=pltpu.CompilerParams(vmem_limit_bytes=4 << 20),
        cost_estimate=pl.CostEstimate(flops=1 << 33, bytes_accessed=32 << 20, transcendentals=0),
    )(
        where_at,
        pltpu.with_memory_space_constraint(atom_counts, pltpu.HBM),
        pltpu.with_memory_space_constraint(atoms, pltpu.HBM),
    )
    across = swapped(sent_across, TOK, 1)
    within = swapped(sent_within, TOK, 0)
    keys = pair.shape[1]
    piece = jax.ShapeDtypeStruct((4, tokens, keys), bf16)
    bias = pl.pallas_call(
        pair_kernel,
        out_shape=(piece, piece, piece, piece),
        in_specs=[pl.BlockSpec(memory_space=pltpu.SMEM), vmem, vmem, hbm],
        out_specs=(vmem, vmem, vmem, vmem),
        scratch_shapes=[pltpu.VMEM((H, tokens, keys), bf16)],
        compiler_params=pltpu.CompilerParams(vmem_limit_bytes=16 << 20),
        cost_estimate=pl.CostEstimate(flops=2 << 30, bytes_accessed=8 << 20, transcendentals=0),
    )(where_at, pair, w_pair_bias.T, sent_across)
    across, within, *bias = lax.optimization_barrier((across, within, *bias))

    width = w_atom.shape[2]
    partial, mix = call(
        atom_kernel,
        (
            jax.ShapeDtypeStruct((tokens, model), bf16),
            jax.ShapeDtypeStruct((width, slots), bf16),
        ),
        (
            where_at,
            atom_counts,
            atom_counts.reshape(1, tokens),
            atoms,
            across,
            within,
            w_atom.transpose(1, 2, 0).reshape(3 * width, channels),
            w_atom_token,
        ),
        [pltpu.VMEM((TAIL + slots + HEADROWS, channels), f32)],
        2,
    )
    quarter = model // 4
    partials = of_everyone(partial)
    partial, *bias = lax.optimization_barrier((partial, *bias))
    bias = [bias[0]] + [sent_around(bias[d], "head", d) for d in (1, 2, 3)]
    residual, kv, query, gate = call(
        projection_kernel,
        (
            jax.ShapeDtypeStruct((tokens, model), f32),
            jax.ShapeDtypeStruct((8, tokens, 2 * quarter), bf16),
            jax.ShapeDtypeStruct((tokens, quarter), bf16),
            jax.ShapeDtypeStruct((tokens, quarter), f32),
        ),
        (
            *partials,
            single,
            ln_gain.reshape(1, model),
            w_proj.transpose(1, 2, 0).reshape(-1, model),
        ),
        [],
        0,
    )
    kv_own = exchanged(kv, "z")
    kv_own, *bias = lax.optimization_barrier((kv_own, *bias))
    kv_own = [kv_own] + [sent_around(kv_own, "x", d) for d in (1, 2, 3)]
    kv_other = [sent_around(piece, "core", 1) for piece in kv_own]
    partial = call(
        attention_kernel,
        jax.ShapeDtypeStruct((tokens, model), bf16),
        (where_at, *kv_own, *kv_other, query, gate, *bias, w_out),
        [
            pltpu.VMEM((8, 4, 2, tokens, 2 * quarter), bf16),
            pltpu.VMEM((4, 4 * tokens, keys), f32),
        ],
        1,
    )
    share, *updates = call(
        tail_kernel,
        (
            jax.ShapeDtypeStruct((tokens, quarter), f32),
            *[jax.ShapeDtypeStruct((tokens, quarter), bf16) for _ in range(3)],
        ),
        (
            where_at,
            *of_everyone(partial),
            residual,
            ln_gain2.reshape(1, model),
            w_trans.transpose(1, 0, 2),
            w_trans_out,
        ),
        [pltpu.VMEM((4, tokens, quarter), f32), pltpu.VMEM((4, tokens, quarter), f32)],
        1,
    )
    updates = [sent_around(u, "head", d) for u, d in zip(updates, (1, 2, 3))]
    refined = (share + sum(u.astype(f32) for u in updates)).astype(bf16)
    return (refined, mix)


def solution(mesh):
    devices = mesh.devices.reshape(8, 4, 2, 4)
    return jax.shard_map(
        shards,
        mesh=Mesh(devices, ("z", "x", "core", "head")),
        in_specs=(
            P(TOK, None),
            P(TOK, "head", None),
            P(TOK, None),
            P(TOK),
            P(None, None, "head"),
            P("head", None),
            P(),
            P(None, None, "head"),
            P(),
            P("head", None),
            P(),
            P(None, None, "head"),
            P("head", None),
        ),
        out_specs=(P(TOK, "head"), P("head", TOK)),
        check_vma=False,
    )
```
